1024 devices in a mesh: pipe: 32 (over z), ctx: 32 (over y, x, core).
Axes of the slice: x: 4, y: 4, z: 32, core: 2. Of those that a mesh axis runs over, the one named last changes fastest.
Arguments:
- segment: bfloat16 [32, 4096, 4096], P('pipe', 'ctx'), may hold values from -6 to 6
- cotangent: bfloat16 [32, 4096, 4096], P('pipe', 'ctx'), may hold values from -6 to 6
- domain: int32 [32, 4096], P('pipe', 'ctx'), may hold values from 0 to 7
- short_filters: float32 [32, 3, 7, 4096], P('pipe'), may hold values from -2.5 to 2.5
- medium_filters: float32 [32, 256, 128], P('pipe'), may hold values from -0.5 to 0.5
Outputs:
- passed_grad: bfloat16 [32, 4096, 4096], P('pipe', 'ctx')
The draws below stay inside these ranges and needn't reach their ends.
All inputs are finite; a program needn't handle non-finite values.
Results may differ from the reference program's by a relative error of at most 0.0064.
Values may be sent and summed in bfloat16 or wider, within the bound.
No kernel may reach another device: no remote copies, remote signals or barrier semaphores. Data moves between devices by JAX's collectives and lax.ppermute only.
A program may use at most 64 MiB of HBM per device.

```python
import jax
import jax.numpy as jnp
import numpy as np
from jax import lax

D = 4096
GROUPS = 256
SHORT = 7
MEDIUM = 128
DOMAINS = 8
TOKENS = 4096
SECTIONS = 32
GSIZE = 16


def place_ends(entries, stream_key, least, high):
    dims = entries.shape
    spot = [jax.random.randint(jax.random.fold_in(stream_key, axis), (), 0, dims[axis]) for axis in range(len(dims))]
    entries = entries.at[tuple(spot)].set(least)
    longest = dims.index(max(dims))
    spot[longest] = (spot[longest] + 1) % dims[longest]
    return entries.at[tuple(spot)].set(high)


def block_levels(rng, extent, shards, smallest, largest):
    level = 1.0
    for axis_at, shards_of in shards:
        heights = jax.random.uniform(jax.random.fold_in(jax.random.fold_in(rng, 6), axis_at), (shards_of,), jnp.float32, smallest / len(shards), largest / len(shards))
        level = level * jnp.repeat(jnp.exp(heights), extent[axis_at] // shards_of).reshape((-1,) + (1,) * (len(extent) - 1 - axis_at))
    return level


def bell_draw(rng, shape, deviation, limit, cuts=(), kind=jnp.bfloat16):
    values = jax.random.normal(rng, shape, jnp.float32) * deviation
    if len(cuts) > 0:
        values = block_levels(rng, shape, cuts, -0.22, 0.18) * values
    return jnp.clip(values, min=-limit, max=limit).astype(kind)


def setup_inputs(seed: int = 0) -> dict:
    streams_of = jax.random.split(jax.random.key(seed), 6)
    segment = bell_draw(streams_of[0], (SECTIONS, TOKENS, D), 1.0, 6.0, ((0, 32), (1, 32)))
    cotangent = bell_draw(streams_of[1], (SECTIONS, TOKENS, D), 1.0, 6.0, ((0, 32), (1, 32)))
    domain = place_ends(jax.random.randint(streams_of[2], (SECTIONS, TOKENS), 0, DOMAINS), jax.random.fold_in(streams_of[2], 1), 0, DOMAINS - 1).astype(jnp.int32)
    short_filters = bell_draw(streams_of[3], (SECTIONS, 3, SHORT, D), 0.4, 2.5, ((0, 32),), jnp.float32)
    medium_filters = bell_draw(streams_of[4], (SECTIONS, GROUPS, MEDIUM), 0.1, 0.5, ((0, 32),), jnp.float32)
    return dict(segment=segment, cotangent=cotangent, domain=domain, short_filters=short_filters, medium_filters=medium_filters)


loss_table = [0.5, 1.0, 1.5, 2.0, 3.0, 0.25, 1.25, 2.5]


def short_causal(signal, taps_short):
    tok_count = signal.shape[0]
    padded = jnp.pad(signal, ((SHORT - 1, 0), (0, 0)))
    total = jnp.zeros(signal.shape, jnp.float32)
    for offset in range(SHORT):
        start = SHORT - 1 - offset
        total = total + taps_short[offset] * padded[start:start + tok_count]
    return total


def short_anticausal(signal, taps_short):
    tok_count = signal.shape[0]
    padded = jnp.pad(signal, ((0, SHORT - 1), (0, 0)))
    total = jnp.zeros(signal.shape, jnp.float32)
    for offset in range(SHORT):
        total = total + taps_short[offset] * padded[offset:offset + tok_count]
    return total


def toeplitz_pair(filters):
    lag_near = np.arange(MEDIUM)[:, None] - np.arange(MEDIUM)[None, :]
    lag_far = lag_near + MEDIUM
    near = jnp.take(filters, np.clip(lag_near, 0, MEDIUM - 1), axis=1)
    far = jnp.take(filters, np.clip(lag_far, 0, MEDIUM - 1), axis=1)
    near = jnp.where(jnp.asarray(lag_near >= 0)[None], near, jnp.zeros_like(near))
    far = jnp.where(jnp.asarray(lag_far <= MEDIUM - 1)[None], far, jnp.zeros_like(far))
    return near, far


def medium_causal(signal, near, far):
    blocks = signal.reshape(-1, MEDIUM, GROUPS, GSIZE)
    earlier = jnp.concatenate([jnp.zeros_like(blocks[:1]), blocks[:-1]], 0)
    hi = lax.Precision.HIGHEST
    out = jnp.einsum("gts,bsgc->btgc", near, blocks, precision=hi)
    out = out + jnp.einsum("gts,bsgc->btgc", far, earlier, precision=hi)
    return out.reshape(signal.shape)


def medium_anticausal(signal, near, far):
    blocks = signal.reshape(-1, MEDIUM, GROUPS, GSIZE)
    later = jnp.concatenate([blocks[1:], jnp.zeros_like(blocks[:1])], 0)
    hi = lax.Precision.HIGHEST
    out = jnp.einsum("gts,btgc->bsgc", near, blocks, precision=hi)
    out = out + jnp.einsum("gts,btgc->bsgc", far, later, precision=hi)
    return out.reshape(signal.shape)


def one_section(packed):
    feats, grads, domain_ids, taps_short, taps_medium = packed
    feats_f = feats.astype(jnp.float32)
    q_stream = short_causal(feats_f, taps_short[0])
    k_stream = short_causal(feats_f, taps_short[1])
    v_stream = short_causal(feats_f, taps_short[2])
    mixed = lax.optimization_barrier((k_stream * v_stream).astype(jnp.bfloat16))
    onehot = domain_ids[:, None] == jnp.arange(DOMAINS, dtype=jnp.int32)[None, :]
    table = jnp.asarray(loss_table, jnp.float32)
    token_weight = jnp.sum(jnp.where(onehot, table[None, :], jnp.zeros((), jnp.float32)), axis=1)
    gated = grads.astype(jnp.float32) * token_weight[:, None]
    conv_grad = lax.optimization_barrier((q_stream * gated).astype(jnp.bfloat16))
    taps_bf = lax.optimization_barrier(taps_medium.astype(jnp.bfloat16))
    near, far = toeplitz_pair(taps_bf.astype(jnp.float32))
    conv_out = medium_causal(mixed.astype(jnp.float32), near, far).astype(jnp.bfloat16)
    mixed_grad = medium_anticausal(conv_grad.astype(jnp.float32), near, far).astype(jnp.bfloat16)
    conv_out = lax.optimization_barrier(conv_out).astype(jnp.float32)
    mixed_grad = lax.optimization_barrier(mixed_grad).astype(jnp.float32)
    grad_query = gated * conv_out
    grad_key = mixed_grad * v_stream
    grad_value = mixed_grad * k_stream
    total = short_anticausal(grad_query, taps_short[0])
    total = total + short_anticausal(grad_key, taps_short[1])
    total = total + short_anticausal(grad_value, taps_short[2])
    return total.astype(jnp.bfloat16)


def reference(segment, cotangent, domain, short_filters, medium_filters):
    input_grad = lax.map(one_section, (segment, cotangent, domain, short_filters, medium_filters))
    return jnp.roll(input_grad, -1, axis=0)
```

```python
import functools

import jax
import jax.numpy as jnp
from jax import lax
from jax.experimental import pallas as pl
from jax.experimental.pallas import tpu as pltpu
from jax.sharding import PartitionSpec as P

SHORT = 7
MEDIUM = 128
GSIZE = 16
LANES = 128
RIM = 8
WIDTH = 256

loss_table = [0.5, 1.0, 1.5, 2.0, 3.0, 0.25, 1.25, 2.5]

HALO_PARTS = (4, 12)
PASS_PARTS = (4, 4, 4, 4)


def ring_pairs(count, by):
    return [(i, i + by) for i in range(count) if 0 <= i + by < count]


def token_weights(domain_ref):
    ids = domain_ref[...]
    row = jnp.zeros(ids.shape, jnp.float32)
    for index, value in enumerate(loss_table):
        row = jnp.where(ids == index, jnp.float32(value), row)
    return jnp.broadcast_to(row, (MEDIUM, MEDIUM)).T


def reversal():
    rows = lax.broadcasted_iota(jnp.int32, (MEDIUM, MEDIUM), 0)
    cols = lax.broadcasted_iota(jnp.int32, (MEDIUM, MEDIUM), 1)
    return (rows + cols == MEDIUM - 1).astype(jnp.float32).astype(jnp.bfloat16)


def identity():
    rows = lax.broadcasted_iota(jnp.int32, (MEDIUM, MEDIUM), 0)
    cols = lax.broadcasted_iota(jnp.int32, (MEDIUM, MEDIUM), 1)
    return (rows == cols).astype(jnp.float32).astype(jnp.bfloat16)


def streams_kernel(seg_ref, rim_ref, cot_ref, domain_ref, short_ref, k_ref, v_ref, mixed_ref, grad_ref):
    weight = token_weights(domain_ref)
    flip = reversal()
    for lane in range(0, seg_ref.shape[2], LANES):
        cols = pl.ds(lane, LANES)
        x = jnp.concatenate(
            [rim_ref[:, cols].astype(jnp.float32), seg_ref[0, :, cols].astype(jnp.float32)], 0
        )
        sums = [None, None, None]
        for j in range(SHORT):
            moved = (x if j == 0 else pltpu.roll(x, j, 0))[RIM:]
            for i in range(3):
                term = short_ref[0, i, j, cols][None, :] * moved
                sums[i] = term if j == 0 else sums[i] + term
        q, k, v = sums
        k_ref[:, cols] = k.astype(jnp.bfloat16)
        v_ref[:, cols] = v.astype(jnp.bfloat16)
        mixed_ref[pl.ds(lane, LANES), :] = (k * v).T.astype(jnp.bfloat16)
        gated = cot_ref[0, :, cols].astype(jnp.float32) * weight
        grad = (q * gated).astype(jnp.bfloat16)
        back = jnp.dot(flip, grad, preferred_element_type=jnp.float32)
        grad_ref[pl.ds(lane, LANES), :] = back.T.astype(jnp.bfloat16)


def grads_kernel(
    taps_ref, mixed_ref, before_ref, grad_ref, after_ref, k_ref, v_ref, cot_ref, domain_ref, short_ref,
    out_ref, own_ref, sent_ref, conv_ref, back_ref,
):
    width = k_ref.shape[1]
    rows = lax.broadcasted_iota(jnp.int32, (MEDIUM, MEDIUM), 0)
    cols = lax.broadcasted_iota(jnp.int32, (MEDIUM, MEDIUM), 1)
    near_mask = cols >= rows
    for g in range(width // GSIZE):
        at = pl.ds(g * GSIZE, GSIZE)
        taps = taps_ref[0, g].astype(jnp.bfloat16).astype(jnp.float32)
        spread = jnp.broadcast_to(taps[None, :], (MEDIUM, MEDIUM))
        circle = pltpu.roll(spread, 0, 1, stride=1, stride_axis=0)
        near = jnp.where(near_mask, circle, 0.0).astype(jnp.bfloat16)
        far = jnp.where(near_mask, 0.0, circle).astype(jnp.bfloat16)
        recent = jnp.concatenate([mixed_ref[at, :], grad_ref[at, :]], 0)
        older = jnp.concatenate([before_ref[at, :], after_ref[at, :]], 0)
        both = jnp.dot(
            jnp.concatenate([older, recent], 1),
            jnp.concatenate([far, near], 0),
            preferred_element_type=jnp.float32,
        ).astype(jnp.bfloat16)
        conv_ref[at, :] = both[:GSIZE]
        back_ref[at, :] = both[GSIZE:]
    weight = token_weights(domain_ref)
    keep, flip = identity(), reversal()
    contract = (((1,), (1,)), ((), ()))
    tail = lax.broadcasted_iota(jnp.int32, (RIM, LANES), 0)
    for lane in range(0, width, LANES):
        at = pl.ds(lane, LANES)
        conv = lax.dot_general(keep, conv_ref[at, :], contract, preferred_element_type=jnp.float32)
        back = lax.dot_general(flip, back_ref[at, :], contract, preferred_element_type=jnp.float32)
        gated = cot_ref[0, :, at].astype(jnp.float32) * weight
        grads = (
            gated * conv,
            back * v_ref[:, at].astype(jnp.float32),
            back * k_ref[:, at].astype(jnp.float32),
        )
        total = own = sent = None
        for j in range(SHORT):
            part = None
            for i in range(3):
                term = short_ref[0, i, j, at][None, :] * grads[i]
                part = term if i == 0 else part + term
            if j == 0:
                total = part
                own = part[MEDIUM - RIM :]
                sent = jnp.zeros_like(own)
                continue
            part = pltpu.roll(part, MEDIUM - j, 0)
            total = total + part
            last = part[MEDIUM - RIM :]
            inside = tail < RIM - j
            own = own + jnp.where(inside, last, 0.0)
            sent = sent + jnp.where(inside, 0.0, last)
        out_ref[:, at] = total[: MEDIUM - RIM].astype(jnp.bfloat16)
        own_ref[:, at] = own
        sent_ref[:, at] = sent


def streams(segment, rim, cotangent, domain, short_filters, start, size):
    first = start // WIDTH
    wide = jax.ShapeDtypeStruct((MEDIUM, size), jnp.bfloat16)
    tall = jax.ShapeDtypeStruct((size, MEDIUM), jnp.bfloat16)
    wide_spec = pl.BlockSpec((MEDIUM, WIDTH), lambda i: (0, i))
    tall_spec = pl.BlockSpec((WIDTH, MEDIUM), lambda i: (i, 0))
    return pl.pallas_call(
        streams_kernel,
        out_shape=(wide, wide, tall, tall),
        grid=(size // WIDTH,),
        in_specs=[
            pl.BlockSpec((1, MEDIUM, WIDTH), lambda i: (0, 0, first + i)),
            pl.BlockSpec((RIM, WIDTH), lambda i: (0, first + i)),
            pl.BlockSpec((1, MEDIUM, WIDTH), lambda i: (0, 0, first + i)),
            pl.BlockSpec((1, MEDIUM), lambda i: (0, 0)),
            pl.BlockSpec((1, 3, SHORT, WIDTH), lambda i: (0, 0, 0, first + i)),
        ],
        out_specs=(wide_spec, wide_spec, tall_spec, tall_spec),
        name=f"streams_{start}",
    )(segment, rim, cotangent, domain, short_filters)


def input_grads(taps, mixed, before, grad, after, k, v, cotangent, domain, short_filters, start, size, base):
    first = start // WIDTH
    near = (start - base) // WIDTH
    groups = WIDTH // GSIZE
    wide_in = pl.BlockSpec((MEDIUM, WIDTH), lambda i: (0, near + i))
    tall_in = pl.BlockSpec((WIDTH, MEDIUM), lambda i: (near + i, 0))
    return pl.pallas_call(
        grads_kernel,
        out_shape=(
            jax.ShapeDtypeStruct((MEDIUM - RIM, size), jnp.bfloat16),
            jax.ShapeDtypeStruct((RIM, size), jnp.float32),
            jax.ShapeDtypeStruct((RIM, size), jnp.float32),
        ),
        grid=(size // WIDTH,),
        in_specs=[
            pl.BlockSpec((1, groups, MEDIUM), lambda i: (0, first + i, 0)),
            tall_in,
            tall_in,
            tall_in,
            tall_in,
            wide_in,
            wide_in,
            pl.BlockSpec((1, MEDIUM, WIDTH), lambda i: (0, 0, first + i)),
            pl.BlockSpec((1, MEDIUM), lambda i: (0, 0)),
            pl.BlockSpec((1, 3, SHORT, WIDTH), lambda i: (0, 0, 0, first + i)),
        ],
        out_specs=(
            pl.BlockSpec((MEDIUM - RIM, WIDTH), lambda i: (0, i)),
            pl.BlockSpec((RIM, WIDTH), lambda i: (0, i)),
            pl.BlockSpec((RIM, WIDTH), lambda i: (0, i)),
        ),
        scratch_shapes=[pltpu.VMEM((WIDTH, MEDIUM), jnp.bfloat16)] * 2,
        name=f"input_grads_{start}",
    )(taps, mixed, before, grad, after, k, v, cotangent, domain, short_filters)


def body(segment, cotangent, domain, short_filters, medium_filters):
    channels = segment.shape[2]
    ctx_count = lax.axis_size("ctx")
    pipe_count = lax.axis_size("pipe")
    onward, backward = ring_pairs(ctx_count, 1), ring_pairs(ctx_count, -1)
    passing = [(i, (i - 1) % pipe_count) for i in range(pipe_count)]
    unit = channels // 16

    rim = lax.ppermute(segment[0, MEDIUM - RIM :], "ctx", onward)
    halos, start = [], 0
    for part in HALO_PARTS:
        size = part * unit
        k, v, mixed, grad = streams(segment, rim, cotangent, domain, short_filters, start, size)
        before = lax.ppermute(mixed, "ctx", onward)
        after = lax.ppermute(grad, "ctx", backward)
        halos.append((start, size, (mixed, before, grad, after, k, v)))
        start += size
    passed, own, sent, start = [], [], [], 0
    for part in PASS_PARTS:
        size = part * unit
        base, _, arrays = next(h for h in halos if h[0] <= start < h[0] + h[1])
        out, own_part, sent_part = input_grads(
            medium_filters, *arrays, cotangent, domain, short_filters, start, size, base
        )
        passed.append((start, lax.ppermute(out, "pipe", passing)))
        own.append(own_part)
        sent.append(sent_part)
        start += size
    received = lax.ppermute(jnp.concatenate(sent, 1), "ctx", backward)
    last = (jnp.concatenate(own, 1) + received).astype(jnp.bfloat16)
    last = lax.ppermute(last, "pipe", passing)
    result = jnp.zeros((MEDIUM, channels), jnp.bfloat16)
    for start, out in passed:
        result = lax.dynamic_update_slice(result, out, (0, start))
    result = lax.dynamic_update_slice(result, last, (MEDIUM - RIM, 0))
    return result[None]


def solution(mesh):
    placed = (
        P("pipe", "ctx", None),
        P("pipe", "ctx", None),
        P("pipe", "ctx"),
        P("pipe", None, None, None),
        P("pipe", None, None),
    )
    return jax.shard_map(
        body, mesh=mesh, in_specs=placed, out_specs=P("pipe", "ctx", None), check_vma=False
    )
```

```python
import jax
import jax.numpy as jnp
from jax import lax
from jax.experimental import pallas as pl
from jax.experimental.pallas import tpu as pltpu
from jax.sharding import PartitionSpec as P


SHORT = 7
MEDIUM = 128
GSIZE = 16
LANES = 128
RIM = 8
WIDTH = 512
ROWS = 32

loss_table = [0.5, 1.0, 1.5, 2.0, 3.0, 0.25, 1.25, 2.5]

HALO_PARTS = (8, 8)
PASS_PARTS = (4, 4, 4, 4)

whole = pl.BlockSpec(memory_space=pltpu.VMEM)


def in_vmem(x):
    return pltpu.with_memory_space_constraint(x, pltpu.VMEM)


def in_hbm(x):
    return pltpu.with_memory_space_constraint(x, pltpu.HBM)


def token_weights(domain_ref):
    ids = domain_ref[...]
    row = jnp.zeros(ids.shape, jnp.float32)
    for index, value in enumerate(loss_table):
        row = jnp.where(ids == index, jnp.float32(value), row)
    return jnp.broadcast_to(row, (MEDIUM, MEDIUM)).T


def square(test):
    rows = lax.broadcasted_iota(jnp.int32, (MEDIUM, MEDIUM), 0)
    cols = lax.broadcasted_iota(jnp.int32, (MEDIUM, MEDIUM), 1)
    return test(rows, cols).astype(jnp.float32).astype(jnp.bfloat16)


def reversal():
    return square(lambda r, c: r + c == MEDIUM - 1)


def identity():
    return square(lambda r, c: r == c)


def streams_kernel(
    parity_ref, seg_ref, rim_ref, cot_ref, domain_ref, short_ref, after_ref,
    k_ref, v_ref, first_ref, second_ref, token_ref, weight_ref, x_ref, mixed_ref, grad_ref, *, start,
):
    step = pl.program_id(0)
    even = parity_ref[0] == 0

    @pl.when(step == 0)
    def _():
        weight_ref[...] = token_weights(domain_ref)
        token_ref[...] = jnp.zeros_like(token_ref)

    flip = reversal()
    for b in range(seg_ref.shape[2] // LANES):
        cols = pl.ds(b * LANES, LANES)
        x_ref[b, :RIM, :] = rim_ref[:, pl.ds(pl.multiple_of(start + step * WIDTH + b * LANES, LANES), LANES)].astype(jnp.float32)
        x_ref[b, RIM:, :] = seg_ref[0, :, cols].astype(jnp.float32)
        out_cols = pl.ds(pl.multiple_of(step * WIDTH + b * LANES, LANES), LANES)
        taps = [[short_ref[i * SHORT + j, :, cols] for j in range(SHORT)] for i in range(3)]
        for r in range(0, MEDIUM, ROWS):
            sums = [None, None, None]
            for j in range(SHORT):
                moved = x_ref[b, pl.ds(RIM + r - j, ROWS), :]
                for i in range(3):
                    term = taps[i][j] * moved
                    sums[i] = term if j == 0 else sums[i] + term
            q, k, v = sums
            rows = pl.ds(r, ROWS)
            k_ref[rows, out_cols] = k.astype(jnp.bfloat16)
            v_ref[rows, out_cols] = v.astype(jnp.bfloat16)
            mixed_ref[b, rows, :] = k * v
            gated = cot_ref[0, rows, cols].astype(jnp.float32) * weight_ref[rows, :]
            grad_ref[b, rows, :] = (q * gated).astype(jnp.bfloat16)
        mixed = mixed_ref[b].T.astype(jnp.bfloat16)
        back = jnp.dot(flip, grad_ref[b], preferred_element_type=jnp.float32)
        grad = back.T.astype(jnp.bfloat16)
        out_rows = pl.ds(pl.multiple_of(step * WIDTH + b * LANES, LANES), LANES)
        first_ref[out_rows, :] = jnp.where(even, mixed, grad)
        second_ref[out_rows, :] = jnp.where(even, grad, mixed)


def toeplitz_kernel(taps_ref, matrix_ref):
    step = pl.program_id(0)
    near_mask = square(lambda r, c: c >= r)
    far_mask = square(lambda r, c: c < r)
    groups = taps_ref.shape[1]
    for g in range(groups):
        taps = taps_ref[0, pl.ds(g, 1), :].astype(jnp.bfloat16).astype(jnp.float32)
        spread = jnp.broadcast_to(taps, (MEDIUM, MEDIUM))
        circle = pltpu.roll(spread, 0, 1, stride=1, stride_axis=0).astype(jnp.bfloat16)
        matrix_ref[step * groups + g, :MEDIUM, :] = circle * far_mask
        matrix_ref[step * groups + g, MEDIUM:, :] = circle * near_mask


def grads_kernel(
    parity_ref, matrix_ref, first_ref, first_got_ref, second_ref, second_got_ref, k_ref, v_ref,
    cot_ref, domain_ref, short_ref, after_ref,
    out_ref, own_ref, sent_ref, weight_ref, part_ref, *, start, base,
):
    step = pl.program_id(0)
    even = parity_ref[0] == 0
    width = cot_ref.shape[2]
    blocks = width // LANES
    per_block = LANES // GSIZE

    @pl.when(step == 0)
    def _():
        weight_ref[...] = token_weights(domain_ref)
        blank = jnp.zeros((RIM, LANES), jnp.float32)
        for b in range(blocks):
            for j in range(SHORT):
                part_ref[b, j, :RIM, :] = blank
                part_ref[b, j, RIM + MEDIUM :, :] = blank

    keep, flip = identity(), reversal()
    contract = (((1,), (1,)), ((), ()))
    here = pl.multiple_of(start - base + step * width, width)
    first_group = start // GSIZE + step * (width // GSIZE)

    def products(b):
        convs, backs = [], []
        for g in range(per_block):
            at = pl.ds(pl.multiple_of(here + b * LANES + g * GSIZE, GSIZE), GSIZE)
            windows = jnp.concatenate(
                [
                    jnp.concatenate([second_got_ref[at, :], first_ref[at, :]], 1),
                    jnp.concatenate([first_got_ref[at, :], second_ref[at, :]], 1),
                ],
                0,
            )
            matrix = matrix_ref[first_group + b * per_block + g]
            both = jnp.dot(windows, matrix, preferred_element_type=jnp.float32).astype(jnp.bfloat16)
            convs.append(jnp.where(even, both[:GSIZE], both[GSIZE:]))
            backs.append(jnp.where(even, both[GSIZE:], both[:GSIZE]))
        return jnp.concatenate(convs, 0), jnp.concatenate(backs, 0)

    coming = products(0)
    for b in range(blocks):
        conv_rows, back_rows = coming
        if b + 1 < blocks:
            coming = products(b + 1)
        at = pl.ds(b * LANES, LANES)
        in_cols = pl.ds(pl.multiple_of(here + b * LANES, LANES), LANES)
        out_cols = pl.ds(pl.multiple_of(step * width + b * LANES, LANES), LANES)
        conv = lax.dot_general(keep, conv_rows, contract, preferred_element_type=jnp.float32)
        back = lax.dot_general(flip, back_rows, contract, preferred_element_type=jnp.float32)
        taps = [[short_ref[i * SHORT + j, :, at] for j in range(SHORT)] for i in range(3)]
        for r in range(0, MEDIUM, ROWS):
            rows = pl.ds(r, ROWS)
            gated = cot_ref[0, rows, at].astype(jnp.float32) * weight_ref[rows, :]
            lag = back[r : r + ROWS]
            grads = (
                gated * conv[r : r + ROWS],
                lag * v_ref[rows, in_cols].astype(jnp.float32),
                lag * k_ref[rows, in_cols].astype(jnp.float32),
            )
            for j in range(SHORT):
                part = taps[0][j] * grads[0] + taps[1][j] * grads[1] + taps[2][j] * grads[2]
                part_ref[b, j, pl.ds(RIM + r, ROWS), :] = part
        sent = part_ref[b, 1, pl.ds(1, RIM), :]
        for j in range(2, SHORT):
            sent = sent + part_ref[b, j, pl.ds(j, RIM), :]
        sent_ref[:, out_cols] = sent
        for r in range(0, MEDIUM, ROWS):
            total = part_ref[b, 0, pl.ds(RIM + r, ROWS), :]
            for j in range(1, SHORT):
                total = total + part_ref[b, j, pl.ds(RIM + r + j, ROWS), :]
            if r + ROWS < MEDIUM:
                out_ref[pl.ds(r, ROWS), out_cols] = total.astype(jnp.bfloat16)
            else:
                out_ref[pl.ds(r, ROWS - RIM), out_cols] = total[: ROWS - RIM].astype(jnp.bfloat16)
                own_ref[:, out_cols] = total[ROWS - RIM :]


def toeplitz(taps):
    _, groups, count = taps.shape
    return pl.pallas_call(
        toeplitz_kernel,
        out_shape=pltpu.VMEM((groups, 2 * count, count), jnp.bfloat16),
        grid=(groups // GSIZE,),
        in_specs=[pl.BlockSpec((1, GSIZE, count), lambda i: (0, i, 0))],
        out_specs=whole,
        compiler_params=pltpu.CompilerParams(vmem_limit_bytes=24 << 20),
        name="toeplitz",
    )(taps)


def streams(parity, segment, rim, cotangent, domain, short, after, start, size):
    first = start // WIDTH
    wide = pltpu.VMEM((MEDIUM, size), jnp.bfloat16)
    tall = pltpu.VMEM((size, MEDIUM), jnp.bfloat16)
    blocks = WIDTH // LANES

    def kernel(*refs):
        streams_kernel(*refs, start=start)

    return pl.pallas_call(
        kernel,
        out_shape=(wide, wide, tall, tall, pltpu.VMEM((RIM, LANES), jnp.float32)),
        grid=(size // WIDTH,),
        in_specs=[
            pl.BlockSpec(memory_space=pltpu.SMEM),
            pl.BlockSpec((1, MEDIUM, WIDTH), lambda i: (0, 0, first + i)),
            whole,
            pl.BlockSpec((1, MEDIUM, WIDTH), lambda i: (0, 0, first + i)),
            pl.BlockSpec((1, MEDIUM), lambda i: (0, 0)),
            pl.BlockSpec((3 * SHORT, 1, WIDTH), lambda i: (0, 0, first + i)),
            whole,
        ],
        out_specs=(whole,) * 5,
        scratch_shapes=[
            pltpu.VMEM((MEDIUM, LANES), jnp.float32),
            pltpu.VMEM((blocks, RIM + MEDIUM, LANES), jnp.float32),
            pltpu.VMEM((blocks, MEDIUM, LANES), jnp.float32),
            pltpu.VMEM((blocks, MEDIUM, LANES), jnp.bfloat16),
        ],
        compiler_params=pltpu.CompilerParams(vmem_limit_bytes=24 << 20),
    )(parity, segment, rim, cotangent, domain, short, after)


def input_grads(parity, matrices, arrays, cotangent, domain, short, after, start, size, base):
    first = start // WIDTH
    blocks = WIDTH // LANES

    def kernel(*refs):
        grads_kernel(*refs, start=start, base=base)

    return pl.pallas_call(
        kernel,
        out_shape=(
            pltpu.VMEM((MEDIUM - RIM, size), jnp.bfloat16),
            pltpu.VMEM((RIM, size), jnp.float32),
            pltpu.VMEM((RIM, size), jnp.float32),
        ),
        grid=(size // WIDTH,),
        in_specs=[
            pl.BlockSpec(memory_space=pltpu.SMEM),
            whole,
            whole,
            whole,
            whole,
            whole,
            whole,
            whole,
            pl.BlockSpec((1, MEDIUM, WIDTH), lambda i: (0, 0, first + i)),
            pl.BlockSpec((1, MEDIUM), lambda i: (0, 0)),
            pl.BlockSpec((3 * SHORT, 1, WIDTH), lambda i: (0, 0, first + i)),
            whole,
        ],
        out_specs=(whole,) * 3,
        scratch_shapes=[
            pltpu.VMEM((MEDIUM, LANES), jnp.float32),
            pltpu.VMEM((blocks, SHORT, MEDIUM + 2 * RIM, LANES), jnp.float32),
        ],
        compiler_params=pltpu.CompilerParams(vmem_limit_bytes=24 << 20),
    )(parity, matrices, *arrays, cotangent, domain, short, after)


def exchange_pairs(count, odd):
    pairs = []
    for low in range(odd, count - 1, 2):
        pairs += [(low, low + 1), (low + 1, low)]
    return pairs


def body(segment, cotangent, domain, short_filters, medium_filters):
    channels = segment.shape[2]
    ctx_count = lax.axis_size("ctx")
    pipe_count = lax.axis_size("pipe")
    onward = [(i, i + 1) for i in range(ctx_count - 1)]
    backward = [(i + 1, i) for i in range(ctx_count - 1)]
    inner, outer = exchange_pairs(ctx_count, 0), exchange_pairs(ctx_count, 1)
    passing = [(i, (i - 1) % pipe_count) for i in range(pipe_count)]
    unit = channels // 16
    parity = jnp.full((1,), lax.axis_index("ctx") % 2, jnp.int32)
    short = jnp.transpose(short_filters, (1, 2, 0, 3)).reshape(3 * SHORT, 1, channels)

    rim = in_vmem(lax.ppermute(segment[0, MEDIUM - RIM :], "ctx", onward))
    segment, cotangent, short, domain, medium_filters = map(
        in_hbm, (segment, cotangent, short, domain, medium_filters)
    )
    matrices = in_vmem(toeplitz(medium_filters))
    halos, start, after = [], 0, rim
    for part in HALO_PARTS:
        size = part * unit
        results = streams(parity, segment, rim, cotangent, domain, short, after, start, size)
        k, v, first, second, after = map(in_vmem, results)
        first_got = in_vmem(lax.ppermute(first, "ctx", inner))
        second_got = in_vmem(lax.ppermute(second, "ctx", outer))
        halos.append((start, size, (first, first_got, second, second_got, k, v)))
        start += size
    passed, own, sent, start = [], [], [], 0
    for part in PASS_PARTS:
        size = part * unit
        base, _, arrays = next(h for h in halos if h[0] <= start < h[0] + h[1])
        out, own_part, sent_part = input_grads(
            parity, matrices, arrays, cotangent, domain, short, after, start, size, base
        )
        passed.append((start, lax.ppermute(out, "pipe", passing)))
        own.append(own_part)
        sent.append(sent_part)
        start += size
        after = in_vmem(own_part)
    received = lax.ppermute(jnp.concatenate(sent, 1), "ctx", backward)
    last = (jnp.concatenate(own, 1) + received).astype(jnp.bfloat16)
    last = lax.ppermute(last, "pipe", passing)
    result = jnp.zeros((MEDIUM, channels), jnp.bfloat16)
    for start, out in passed:
        result = lax.dynamic_update_slice(result, out, (0, start))
    result = lax.dynamic_update_slice(result, last, (MEDIUM - RIM, 0))
    return result[None]


def solution(mesh):
    placed = (
        P("pipe", "ctx", None),
        P("pipe", "ctx", None),
        P("pipe", "ctx"),
        P("pipe", None, None, None),
        P("pipe", None, None),
    )

    return jax.shard_map(
        body, mesh=mesh, in_specs=placed, out_specs=P("pipe", "ctx", None), check_vma=False
    )
```

```python
import jax
import jax.numpy as jnp
from jax import lax
from jax.experimental import pallas as pl
from jax.experimental.pallas import tpu as pltpu
from jax.sharding import PartitionSpec as P


SHORT = 7
MEDIUM = 128
GSIZE = 16
GROUPS_A_STEP = 64
LANES = 128
RIM = 8
WIDTH = 512
ROWS = 32

loss_table = [0.5, 1.0, 1.5, 2.0, 3.0, 0.25, 1.25, 2.5]

HALO_PARTS = (10, 6)
PASS_PARTS = (4, 6, 6)

whole = pl.BlockSpec(memory_space=pltpu.VMEM)


def in_vmem(x):
    return pltpu.with_memory_space_constraint(x, pltpu.VMEM)


def in_hbm(x):
    return pltpu.with_memory_space_constraint(x, pltpu.HBM)


def token_weights(domain_ref):
    ids = domain_ref[...]
    row = jnp.zeros(ids.shape, jnp.float32)
    for index, value in enumerate(loss_table):
        row = jnp.where(ids == index, jnp.float32(value), row)
    return jnp.broadcast_to(row, (MEDIUM, MEDIUM)).T


def square(test):
    rows = lax.broadcasted_iota(jnp.int32, (MEDIUM, MEDIUM), 0)
    cols = lax.broadcasted_iota(jnp.int32, (MEDIUM, MEDIUM), 1)
    return test(rows, cols).astype(jnp.float32).astype(jnp.bfloat16)


def reversal():
    return square(lambda r, c: r + c == MEDIUM - 1)


def identity():
    return square(lambda r, c: r == c)


def streams_kernel(
    parity_ref, seg_ref, rim_ref, cot_ref, domain_ref, short_ref, after_ref,
    *refs, start,
):
    k_ref, v_ref, first_ref, second_ref, token_ref, weight_ref, x_ref, mixed_ref, grad_ref = refs[-9:]
    step = pl.program_id(0)
    even = parity_ref[0] == 0

    @pl.when(step == 0)
    def _():
        weight_ref[...] = token_weights(domain_ref)
        token_ref[...] = jnp.zeros_like(token_ref)
        if start > 0:
            first_ref[:start, :] = refs[0][:start, :]

    flip = reversal()
    for b in range(seg_ref.shape[2] // LANES):
        cols = pl.ds(b * LANES, LANES)
        x_ref[b, :RIM, :] = rim_ref[:, pl.ds(pl.multiple_of(start + step * WIDTH + b * LANES, LANES), LANES)].astype(jnp.float32)
        x_ref[b, RIM:, :] = seg_ref[0, :, cols].astype(jnp.float32)
        out_cols = pl.ds(pl.multiple_of(step * WIDTH + b * LANES, LANES), LANES)
        taps = [[short_ref[i * SHORT + j, :, cols] for j in range(SHORT)] for i in range(3)]
        for r in range(0, MEDIUM, ROWS):
            sums = [None, None, None]
            for j in range(SHORT):
                moved = x_ref[b, pl.ds(RIM + r - j, ROWS), :]
                for i in range(3):
                    term = taps[i][j] * moved
                    sums[i] = term if j == 0 else sums[i] + term
            q, k, v = sums
            rows = pl.ds(r, ROWS)
            k_ref[rows, out_cols] = k.astype(jnp.bfloat16)
            v_ref[rows, out_cols] = v.astype(jnp.bfloat16)
            mixed_ref[b, rows, :] = k * v
            gated = cot_ref[0, rows, cols].astype(jnp.float32) * weight_ref[rows, :]
            grad_ref[b, rows, :] = (q * gated).astype(jnp.bfloat16)
        mixed = mixed_ref[b].T.astype(jnp.bfloat16)
        back = jnp.dot(flip, grad_ref[b], preferred_element_type=jnp.float32)
        grad = back.T.astype(jnp.bfloat16)
        out_rows = pl.ds(pl.multiple_of(step * WIDTH + b * LANES, LANES), LANES)
        all_rows = pl.ds(pl.multiple_of(start + step * WIDTH + b * LANES, LANES), LANES)
        first_ref[all_rows, :] = jnp.where(even, mixed, grad)
        second_ref[out_rows, :] = jnp.where(even, grad, mixed)


def toeplitz_kernel(taps_ref, matrix_ref):
    step = pl.program_id(0)
    near_mask = square(lambda r, c: c >= r)
    far_mask = square(lambda r, c: c < r)
    groups = taps_ref.shape[1]
    for g in range(groups):
        taps = taps_ref[0, pl.ds(g, 1), :].astype(jnp.bfloat16).astype(jnp.float32)
        spread = jnp.broadcast_to(taps, (MEDIUM, MEDIUM))
        circle = pltpu.roll(spread, 0, 1, stride=1, stride_axis=0).astype(jnp.bfloat16)
        matrix_ref[step * groups + g, :MEDIUM, :] = circle * far_mask
        matrix_ref[step * groups + g, MEDIUM:, :] = circle * near_mask


def grads_kernel(
    parity_ref, matrix_ref, first_ref, first_got_ref, second_ref, second_got_ref, k_ref, v_ref,
    cot_ref, domain_ref, short_ref, after_ref,
    out_ref, own_ref, sent_ref, weight_ref, part_ref, *, start, base,
):
    step = pl.program_id(0)
    even = parity_ref[0] == 0
    width = cot_ref.shape[2]
    blocks = width // LANES
    per_block = LANES // GSIZE

    @pl.when(step == 0)
    def _():
        weight_ref[...] = token_weights(domain_ref)
        blank = jnp.zeros((RIM, LANES), jnp.float32)
        for b in range(blocks):
            for j in range(SHORT):
                part_ref[b, j, :RIM, :] = blank
                part_ref[b, j, RIM + MEDIUM :, :] = blank

    keep, flip = identity(), reversal()
    contract = (((1,), (1,)), ((), ()))
    here = pl.multiple_of(start - base + step * width, width)
    first_group = start // GSIZE + step * (width // GSIZE)

    def products(b):
        convs, backs = [], []
        for g in range(per_block):
            at = pl.ds(pl.multiple_of(here + b * LANES + g * GSIZE, GSIZE), GSIZE)
            full = pl.ds(pl.multiple_of(start + step * width + b * LANES + g * GSIZE, GSIZE), GSIZE)
            windows = jnp.concatenate(
                [
                    jnp.concatenate([second_got_ref[at, :], first_ref[full, :]], 1),
                    jnp.concatenate([first_got_ref[full, :], second_ref[at, :]], 1),
                ],
                0,
            )
            matrix = matrix_ref[first_group + b * per_block + g]
            both = jnp.dot(windows, matrix, preferred_element_type=jnp.float32).astype(jnp.bfloat16)
            convs.append(jnp.where(even, both[:GSIZE], both[GSIZE:]))
            backs.append(jnp.where(even, both[GSIZE:], both[:GSIZE]))
        return jnp.concatenate(convs, 0), jnp.concatenate(backs, 0)

    coming = products(0)
    for b in range(blocks):
        conv_rows, back_rows = coming
        if b + 1 < blocks:
            coming = products(b + 1)
        at = pl.ds(b * LANES, LANES)
        in_cols = pl.ds(pl.multiple_of(here + b * LANES, LANES), LANES)
        out_cols = pl.ds(pl.multiple_of(step * width + b * LANES, LANES), LANES)
        conv = lax.dot_general(keep, conv_rows, contract, preferred_element_type=jnp.float32)
        back = lax.dot_general(flip, back_rows, contract, preferred_element_type=jnp.float32)
        taps = [[short_ref[i * SHORT + j, :, at] for j in range(SHORT)] for i in range(3)]
        for r in range(0, MEDIUM, ROWS):
            rows = pl.ds(r, ROWS)
            gated = cot_ref[0, rows, at].astype(jnp.float32) * weight_ref[rows, :]
            lag = back[r : r + ROWS]
            grads = (
                gated * conv[r : r + ROWS],
                lag * v_ref[rows, in_cols].astype(jnp.float32),
                lag * k_ref[rows, in_cols].astype(jnp.float32),
            )
            for j in range(SHORT):
                part = taps[0][j] * grads[0] + taps[1][j] * grads[1] + taps[2][j] * grads[2]
                part_ref[b, j, pl.ds(RIM + r, ROWS), :] = part
        sent = part_ref[b, 1, pl.ds(1, RIM), :]
        for j in range(2, SHORT):
            sent = sent + part_ref[b, j, pl.ds(j, RIM), :]
        sent_ref[:, out_cols] = sent
        for r in range(0, MEDIUM, ROWS):
            total = part_ref[b, 0, pl.ds(RIM + r, ROWS), :]
            for j in range(1, SHORT):
                total = total + part_ref[b, j, pl.ds(RIM + r + j, ROWS), :]
            if r + ROWS < MEDIUM:
                out_ref[pl.ds(r, ROWS), out_cols] = total.astype(jnp.bfloat16)
            else:
                out_ref[pl.ds(r, ROWS - RIM), out_cols] = total[: ROWS - RIM].astype(jnp.bfloat16)
                own_ref[:, out_cols] = total[ROWS - RIM :]


def toeplitz(taps):
    _, groups, count = taps.shape
    a_step = min(groups, GROUPS_A_STEP)
    return pl.pallas_call(
        toeplitz_kernel,
        out_shape=pltpu.VMEM((groups, 2 * count, count), jnp.bfloat16),
        grid=(groups // a_step,),
        in_specs=[pl.BlockSpec((1, a_step, count), lambda i: (0, i, 0))],
        out_specs=whole,
        compiler_params=pltpu.CompilerParams(vmem_limit_bytes=24 << 20),
        name="toeplitz",
    )(taps)


def streams(parity, segment, rim, cotangent, domain, short, after, shared, start, size):
    first = start // WIDTH
    blocks = WIDTH // LANES
    wide = pltpu.VMEM((MEDIUM, size), jnp.bfloat16)
    tall = pltpu.VMEM((size, MEDIUM), jnp.bfloat16)
    full = pltpu.VMEM((segment.shape[2], MEDIUM), jnp.bfloat16)
    token = pltpu.VMEM((RIM, LANES), jnp.float32)

    def kernel(*refs):
        streams_kernel(*refs, start=start)

    operands = [parity, segment, rim, cotangent, domain, short, after]
    specs = [
        pl.BlockSpec(memory_space=pltpu.SMEM),
        pl.BlockSpec((1, MEDIUM, WIDTH), lambda i: (0, 0, first + i)),
        whole,
        pl.BlockSpec((1, MEDIUM, WIDTH), lambda i: (0, 0, first + i)),
        pl.BlockSpec((1, MEDIUM), lambda i: (0, 0)),
        pl.BlockSpec((3 * SHORT, 1, WIDTH), lambda i: (0, 0, first + i)),
        whole,
    ]
    if shared is not None:
        operands.append(shared)
        specs.append(whole)
    return pl.pallas_call(
        kernel,
        out_shape=(wide, wide, full, tall, token),
        grid=(size // WIDTH,),
        in_specs=specs,
        out_specs=(whole,) * 5,
        scratch_shapes=[
            pltpu.VMEM((MEDIUM, LANES), jnp.float32),
            pltpu.VMEM((blocks, RIM + MEDIUM, LANES), jnp.float32),
            pltpu.VMEM((blocks, MEDIUM, LANES), jnp.float32),
            pltpu.VMEM((blocks, MEDIUM, LANES), jnp.bfloat16),
        ],
        compiler_params=pltpu.CompilerParams(vmem_limit_bytes=24 << 20),
    )(*operands)


def input_grads(parity, matrices, arrays, cotangent, domain, short, after, start, size, base):
    first = start // WIDTH
    blocks = WIDTH // LANES

    def kernel(*refs):
        grads_kernel(*refs, start=start, base=base)

    return pl.pallas_call(
        kernel,
        out_shape=(
            pltpu.VMEM((MEDIUM - RIM, size), jnp.bfloat16),
            pltpu.VMEM((RIM, size), jnp.float32),
            pltpu.VMEM((RIM, size), jnp.float32),
        ),
        grid=(size // WIDTH,),
        in_specs=[
            pl.BlockSpec(memory_space=pltpu.SMEM),
            whole,
            whole,
            whole,
            whole,
            whole,
            whole,
            whole,
            pl.BlockSpec((1, MEDIUM, WIDTH), lambda i: (0, 0, first + i)),
            pl.BlockSpec((1, MEDIUM), lambda i: (0, 0)),
            pl.BlockSpec((3 * SHORT, 1, WIDTH), lambda i: (0, 0, first + i)),
            whole,
        ],
        out_specs=(whole,) * 3,
        scratch_shapes=[
            pltpu.VMEM((MEDIUM, LANES), jnp.float32),
            pltpu.VMEM((blocks, SHORT, MEDIUM + 2 * RIM, LANES), jnp.float32),
        ],
        compiler_params=pltpu.CompilerParams(vmem_limit_bytes=24 << 20),
    )(parity, matrices, *arrays, cotangent, domain, short, after)


def exchange_pairs(count, odd):
    pairs = []
    for low in range(odd, count - 1, 2):
        pairs += [(low, low + 1), (low + 1, low)]
    return pairs


def body(segment, cotangent, domain, short_filters, medium_filters):
    channels = segment.shape[2]
    ctx_count = lax.axis_size("ctx")
    pipe_count = lax.axis_size("pipe")
    onward = [(i, i + 1) for i in range(ctx_count - 1)]
    backward = [(i + 1, i) for i in range(ctx_count - 1)]
    inner, outer = exchange_pairs(ctx_count, 0), exchange_pairs(ctx_count, 1)
    passing = [(i, (i - 1) % pipe_count) for i in range(pipe_count)]
    unit = channels // 16
    parity = jnp.full((1,), lax.axis_index("ctx") % 2, jnp.int32)
    short = jnp.transpose(short_filters, (1, 2, 0, 3)).reshape(3 * SHORT, 1, channels)

    rim = in_vmem(lax.ppermute(segment[0, MEDIUM - RIM :], "ctx", onward))
    segment, cotangent, short, domain, medium_filters = map(
        in_hbm, (segment, cotangent, short, domain, medium_filters)
    )
    matrices = in_vmem(toeplitz(medium_filters))
    halos, start, after, first = [], 0, rim, None
    for part in HALO_PARTS:
        size = part * unit
        results = streams(parity, segment, rim, cotangent, domain, short, after, first, start, size)
        k, v, first, second, after = map(in_vmem, results)
        second_got = in_vmem(lax.ppermute(second, "ctx", outer))
        halos.append((start, size, (second, second_got, k, v)))
        start += size
    first_got = in_vmem(lax.ppermute(first, "ctx", inner))
    passed, own, sent, start = [], [], [], 0
    for part in PASS_PARTS:
        size = part * unit
        base, _, arrays = next(h for h in halos if h[0] <= start < h[0] + h[1])
        out, own_part, sent_part = input_grads(
            parity, matrices, (first, first_got, *arrays), cotangent, domain, short, after, start, size, base
        )
        passed.append((start, lax.ppermute(out, "pipe", passing)))
        own.append(own_part)
        sent.append(sent_part)
        start += size
        after = in_vmem(own_part)
    received = lax.ppermute(jnp.concatenate(sent, 1), "ctx", backward)
    last = (jnp.concatenate(own, 1) + received).astype(jnp.bfloat16)
    last = lax.ppermute(last, "pipe", passing)
    result = jnp.zeros((MEDIUM, channels), jnp.bfloat16)
    for start, out in passed:
        result = lax.dynamic_update_slice(result, out, (0, start))
    result = lax.dynamic_update_slice(result, last, (MEDIUM - RIM, 0))
    return result[None]


def solution(mesh):
    placed = (
        P("pipe", "ctx", None),
        P("pipe", "ctx", None),
        P("pipe", "ctx"),
        P("pipe", None, None, None),
        P("pipe", None, None),
    )

    return jax.shard_map(
        body, mesh=mesh, in_specs=placed, out_specs=P("pipe", "ctx", None), check_vma=False
    )
```
